32 devices in a mesh: row: 4 (over x, core), col: 8 (over z, y).
Axes of the slice: x: 2, y: 2, z: 4, core: 2. Of those that a mesh axis runs over, the one named last changes fastest.
Arguments:
- front: bfloat16 [24576, 24576], P('row', 'col'), may hold values from -6 to 6
- diag_inverse: bfloat16 [256, 256], replicated, as said below
- fill_pattern: int32 [384, 384], replicated, may hold values from 0 to 1, as said below
Outputs:
- updated: bfloat16 [24576, 24576], P('row', 'col')
The draws below stay inside these ranges and needn't reach their ends.
Inputs may be any that keep to these rules, and one draw needn't show every extreme that they name: `fill_pattern`: symmetric, with ones on the diagonal. `diag_inverse`: lower triangular.
All inputs are finite; a program needn't handle non-finite values.
Results may differ from the reference program's by a relative error of at most 0.0045.
Values may be sent and summed in bfloat16 or wider, within the bound.
A program may use at most 128 MiB of HBM per device.

```python
import jax
import jax.numpy as jnp
from jax import lax

M = 24576
B = 64
P_SIZE = 256
N_ROW = 4
N_COL = 8


def draw_fill_pattern(key, part):
    count = M // B
    values = jax.random.randint(key, (count, count), 0, 4)
    marks = (values < 3).astype(jnp.int32)
    both = marks * marks.T
    ident = jnp.eye(count, dtype=jnp.int32)
    return jnp.maximum(both, ident)


def draw_diag_inverse(key, part):
    first = jax.random.fold_in(key, 0)
    values = jax.random.normal(first, (P_SIZE, P_SIZE), jnp.float32)
    scales = jnp.ones((P_SIZE, 1), jnp.float32)
    index = jnp.arange(P_SIZE, dtype=jnp.int32)
    lower = (index[:, None] >= index[None, :]).astype(jnp.float32)
    counts = (index + 1).astype(jnp.float32)[:, None]
    weights = 0.25 * scales * values * lower / jnp.sqrt(counts)
    weights = weights + 0.2 * jnp.eye(P_SIZE, dtype=jnp.float32)
    return weights.astype(jnp.bfloat16)


def block_levels(stream_key, shape, shards, least, high):
    def one(position, parts):
        heights = jax.random.uniform(jax.random.fold_in(jax.random.fold_in(stream_key, 6), position), (parts,), jnp.float32, least / len(shards), high / len(shards))
        return jnp.repeat(jnp.exp(heights), shape[position] // parts).reshape((-1,) + (1,) * (len(shape) - position - 1))

    loudness = one(*shards[0])
    for cut in shards[1:]:
        loudness = loudness * one(*cut)
    return loudness


def bell_draw(key, shape, scale, limit, cuts=(), held_as=jnp.bfloat16):
    loudness = block_levels(key, shape, cuts, -0.22, 0.18) if cuts else 1.0
    result = jax.random.normal(key, shape, jnp.float32) * scale * loudness
    return jnp.minimum(jnp.maximum(result, -limit), limit).astype(held_as)


def setup_inputs(seed: int = 0) -> dict:
    streams_of = jax.random.split(jax.random.key(seed), 4)
    front = bell_draw(streams_of[0], (M, M), 1.0, 6.0, ((0, 4), (1, 8)))
    diag_inverse = draw_diag_inverse(jax.random.fold_in(streams_of[3], 71), 0)
    fill_pattern = draw_fill_pattern(jax.random.fold_in(streams_of[3], 71), 0)
    return dict(front=front, diag_inverse=diag_inverse, fill_pattern=fill_pattern)


def reference(front, diag_inverse, fill_pattern):
    blocks = M // B
    local_rows = M // (B * N_ROW)
    local_cols = M // (B * N_COL)
    panel_blocks = P_SIZE // B
    stored = jnp.arange(blocks, dtype=jnp.int32)
    row_global = (stored % local_rows) * N_ROW + stored // local_rows
    col_global = (stored % local_cols) * N_COL + stored // local_cols
    panel = jnp.concatenate([front[:, h * local_cols * B:h * local_cols * B + B] for h in range(panel_blocks)], axis=1)
    factor = jnp.dot(panel, diag_inverse.T, preferred_element_type=jnp.float32).astype(jnp.bfloat16)
    source = (col_global % N_ROW) * local_rows + col_global // N_ROW
    col_factor = factor.reshape(blocks, B, P_SIZE)[source].reshape(M, P_SIZE)
    keep = fill_pattern[row_global][:, col_global].astype(jnp.float32)
    keep = keep * (row_global >= panel_blocks).astype(jnp.float32)[:, None]
    keep = keep * (col_global >= panel_blocks).astype(jnp.float32)[None, :]

    def one_block(items):
        front_rows, factor_rows, keep_row = items
        product = jnp.dot(factor_rows, col_factor.T, preferred_element_type=jnp.float32)
        spread = jnp.repeat(keep_row, B)
        return (front_rows.astype(jnp.float32) - product * spread[None, :]).astype(jnp.bfloat16)

    updated = lax.map(one_block, (front.reshape(blocks, B, M), factor.reshape(blocks, B, P_SIZE), keep))
    updated = updated.reshape(M, M)
    for h in range(panel_blocks):
        updated = updated.at[:, h * local_cols * B:h * local_cols * B + B].set(factor[:, h * B:(h + 1) * B])
    return updated
```

```python
import functools

import jax
import jax.numpy as jnp
from jax import lax
from jax.experimental import pallas as pl
from jax.experimental.pallas import tpu as pltpu
from jax.sharding import PartitionSpec as P

B = 64
P_SIZE = 256
LANES = 128
SUPERS = 3
AHEAD = 4
CHAIN = 1
SLOTS = 4
MESH = pl.DeviceIdType.MESH
NT = (((1,), (1,)), ((), ()))


def nt_dot(a, b):
    return lax.dot_general(a, b, NT, preferred_element_type=jnp.float32)


def nn_dot(a, b):
    return jnp.dot(a, b, preferred_element_type=jnp.float32)


def one_hot(shape, test):
    i = lax.broadcasted_iota(jnp.int32, shape, 0)
    j = lax.broadcasted_iota(jnp.int32, shape, 1)
    return jnp.where(test(i, j), 1.0, 0.0).astype(jnp.bfloat16)


def aligned(i, size):
    return pl.ds(pl.multiple_of(i * size, size), size)


def new_tile(held, fac, colf, keep, rows_at, cols_at, step_rows, wide):
    step_blocks = step_rows // B
    product = nn_dot(fac[rows_at, :], colf[:, cols_at])
    marks = keep
    masked = product.reshape(step_blocks, B, wide) * marks[:, None, :]
    value = held[rows_at, cols_at].astype(jnp.float32) - masked.reshape(step_rows, wide)
    return value.astype(jnp.bfloat16)


def head_lanes(fac_rows, old, c):
    to_front = one_hot((P_SIZE, LANES), lambda i, l: (i == c * B + l) & (l < B))
    piece = nn_dot(fac_rows, to_front)
    lane = lax.broadcasted_iota(jnp.int32, old.shape, 1)
    return jnp.where(lane < B, piece, old.astype(jnp.float32)).astype(jnp.bfloat16)


def gather_kernel(
    n_row, n_col,
    front, diag, fill, out, fac, colf, keep,
    source, pan, colp, w_lo, w_hi, picked,
    load_sem, source_sem, row_recv, row_send, col_recv, col_send,
):
    r = lax.axis_index("row")
    c = lax.axis_index("col")
    rows, cols = out.shape
    heads = P_SIZE // B
    ratio = n_col // n_row
    sub_rows = 2 * ratio * B
    step_rows = 2 * sub_rows
    step_cols = step_rows // ratio
    half = sub_rows
    chunks = rows // step_rows
    subs = 2 * chunks
    group = chunks // SUPERS
    wide = cols // SUPERS
    outer, inner = 4, n_col // 4
    a = c // inner
    b = c % inner
    owner = c < heads
    x, core = r // 2, r % 2
    source_row = c % n_row
    source_x, source_core = source_row // 2, source_row % 2
    parity = c // n_row
    n_x = n_row // 2
    is_source = r == source_row
    is_relay = jnp.logical_and(core == source_core, x != source_x)

    def load(k):
        part = aligned(k, step_rows)
        return pltpu.make_async_copy(front.at[part], out.at[part], load_sem.at[k])

    first = min(2, chunks)

    def fetch(part):
        size = (first, chunks - first)[part] * step_rows
        at = pl.ds(part * first * step_rows, size)
        return pltpu.make_async_copy(
            front.at[at, 0:LANES], source.at[at], source_sem.at[part]
        )

    def row_copy(h, ref, recv, slot, target):
        return pltpu.make_async_remote_copy(
            src_ref=ref, dst_ref=ref,
            send_sem=row_send.at[h, slot], recv_sem=recv,
            device_id=(r, target), device_id_type=MESH,
        )

    def row_sends(h, ref, recv, act):
        a_h, b_h = h // inner, h % inner

        @pl.when(b == b_h)
        def _():
            @pl.when(jnp.logical_and(a >= a_h, a < outer - 1))
            def _():
                act(row_copy(h, ref, recv, 0, c + inner))

            @pl.when(jnp.logical_and(a <= a_h, a > 0))
            def _():
                act(row_copy(h, ref, recv, 1, c - inner))

            for d in range(1, inner):
                act(row_copy(h, ref, recv, 1 + d, a * inner + (b + d) % inner))

    def start(copy):
        copy.start()

    def own(s):
        for h in range(heads):
            @pl.when(c == h)
            def _():
                row_sends(h, pan.at[h, s], row_recv.at[h, s], start)

    def chain(s):
        for h in range(heads):
            @pl.when(jnp.logical_and(c != h, b == h % inner))
            def _():
                row_copy(h, pan.at[h, s], row_recv.at[h, s], 0, c).wait_recv()
                row_sends(h, pan.at[h, s], row_recv.at[h, s], start)

    def across(s):
        for h in range(heads):
            @pl.when(b != h % inner)
            def _():
                row_copy(h, pan.at[h, s], row_recv.at[h, s], 0, c).wait_recv()

    def col_copy(src, dst, recv, slot, target):
        return pltpu.make_async_remote_copy(
            src_ref=src, dst_ref=dst,
            send_sem=col_send.at[slot], recv_sem=recv,
            device_id=(target, c), device_id_type=MESH,
        )

    def col_local(s):
        return pltpu.make_async_copy(pan.at[:, s, parity], colp.at[s], col_recv.at[s])

    def col_source(s):
        @pl.when(is_source)
        def _():
            src = pan.at[:, s, parity]
            for d in range(1, n_x):
                target = ((x + d) % n_x) * 2 + core
                col_copy(src, colp.at[s], col_recv.at[s], d, target).start()
            col_copy(src, colp.at[s], col_recv.at[s], 0, x * 2 + 1 - core).start()
            col_local(s).start()

    def col_relay(s):
        @pl.when(is_relay)
        def _():
            copy = col_copy(colp.at[s], colp.at[s], col_recv.at[s], 0, x * 2 + 1 - core)
            copy.wait_recv()
            copy.start()

    def col_wait(s):
        @pl.when(is_source)
        def _():
            col_local(s).wait()

        @pl.when(jnp.logical_not(jnp.logical_or(is_source, is_relay)))
        def _():
            col_copy(colp.at[s], colp.at[s], col_recv.at[s], 0, r).wait_recv()

    @pl.when(owner)
    def _():
        fetch(0).start()
        fetch(1).start()

    for k in range(chunks):
        load(k).start()

    barrier = pltpu.get_barrier_semaphore()

    @pl.when(a > 0)
    def _():
        pl.semaphore_signal(barrier, inc=1, device_id=(r, c - inner), device_id_type=MESH)

    @pl.when(a < outer - 1)
    def _():
        pl.semaphore_signal(barrier, inc=1, device_id=(r, c + inner), device_id_type=MESH)

    for d in range(1, inner):
        pl.semaphore_signal(
            barrier, inc=1, device_id=(r, a * inner + (b + d) % inner), device_id_type=MESH
        )
    for d in range(1, n_row):
        pl.semaphore_signal(barrier, inc=1, device_id=((r + d) % n_row, c), device_id_type=MESH)

    to_lo = one_hot((LANES, LANES), lambda i, j: (i == j) & (i < B))
    to_hi = one_hot((LANES, LANES), lambda i, j: (i + B == j) & (i < B))

    def pack(k, _):
        at = pl.multiple_of(k * step_rows, step_rows)
        both = nn_dot(source[pl.ds(at, half), :], to_lo)
        both += nn_dot(source[pl.ds(at + half, half), :], to_hi)
        both = both.astype(jnp.bfloat16).reshape(2, ratio, B, LANES)
        pan[c, 2 * k] = both[0]
        pan[c, 2 * k + 1] = both[1]
        return 0

    @pl.when(owner)
    def _():
        fetch(0).wait()
        lax.fori_loop(0, first, pack, 0)

    extra = jnp.where(a > 0, 1, 0) + jnp.where(a < outer - 1, 1, 0)
    pl.semaphore_wait(barrier, inner - 1 + n_row - 1 + extra)

    ahead = min(AHEAD, 2 * first)
    for s in range(ahead):
        own(s)

    @pl.when(owner)
    def _():
        fetch(1).wait()
        lax.fori_loop(first, chunks, pack, 0)

    for s in range(CHAIN):
        chain(s)

    def spread(shift):
        return one_hot(
            (P_SIZE, heads * LANES),
            lambda i, j: (i == (j // LANES) * B + j % LANES - shift)
            & (j % LANES >= shift) & (j % LANES < shift + B),
        )

    w_lo[...] = nn_dot(diag[...], spread(0)).astype(jnp.bfloat16)
    w_hi[...] = nn_dot(diag[...], spread(B)).astype(jnp.bfloat16)

    count = fill.shape[0]
    local_rows = rows // B
    pick = one_hot((local_rows, count), lambda i, j: j == i * n_row + r)
    picked[...] = nn_dot(pick, fill[...].astype(jnp.float32).astype(jnp.bfloat16)).astype(
        jnp.bfloat16
    )

    step_blocks = step_rows // B

    def event(s):
        @pl.when(s + ahead < subs)
        def _():
            own(s + ahead)

        @pl.when(s + CHAIN < subs)
        def _():
            chain(s + CHAIN)

        across(s)
        col_source(s)

        @pl.when(s >= 2)
        def _():
            col_relay(s - 2)

    def row_factors(k):
        packed = jnp.concatenate(
            [pan[h, pl.ds(2 * k, 2)].reshape(half, LANES) for h in range(heads)], axis=1
        )
        at = pl.multiple_of(k * step_rows, step_rows)
        fac[pl.ds(at, half), :] = nt_dot(packed, w_lo[...]).astype(jnp.bfloat16)
        fac[pl.ds(at + half, half), :] = nt_dot(packed, w_hi[...]).astype(jnp.bfloat16)

    def col_factors(k):
        col_wait(2 * k)
        col_wait(2 * k + 1)
        packed = jnp.concatenate(
            [colp[pl.ds(2 * k, 2), h].reshape(2 * B, LANES) for h in range(heads)], axis=1
        )
        at = pl.multiple_of(k * step_cols, step_cols)
        colf[:, pl.ds(at, 2 * B)] = nt_dot(w_lo[...], packed).astype(jnp.bfloat16)
        colf[:, pl.ds(at + 2 * B, 2 * B)] = nt_dot(w_hi[...], packed).astype(jnp.bfloat16)

    def make_keep(j):
        at = pl.multiple_of(j * step_cols, step_cols)
        widen = one_hot(
            (count, step_cols), lambda i, l: i == ((at + l) // B) * n_col + c
        )
        marks = nn_dot(picked[...], widen)
        i = lax.broadcasted_iota(jnp.int32, marks.shape, 0)
        l = lax.broadcasted_iota(jnp.int32, marks.shape, 1)
        live = (i * n_row + r >= heads) & (((at + l) // B) * n_col + c >= heads)
        keep[:, pl.ds(at, step_cols)] = jnp.where(live, marks, 0.0)

    def tile(i, j):
        rows_at, cols_at = aligned(i, step_rows), aligned(j, wide)
        marks = keep[aligned(i, step_blocks), cols_at]
        out[rows_at, cols_at] = new_tile(
            out, fac, colf, marks, rows_at, cols_at, step_rows, wide
        )

        @pl.when(jnp.logical_and(owner, j == 0))
        def _():
            out[rows_at, 0:LANES] = head_lanes(fac[rows_at, :], out[rows_at, 0:LANES], c)

    def tiles(k):
        q = k // group
        t = k % group

        def one(m, _):
            fresh = m < q
            i = jnp.where(fresh, k, t * q + m - q)
            j = jnp.where(fresh, m, q - 1)
            tile(i, j)
            return 0

        lax.fori_loop(0, 2 * q, one, 0)

    def step(k, _):
        event(2 * k)

        @pl.when(k > 0)
        def _():
            row_factors(k - 1)

        make_keep(k)
        event(2 * k + 1)

        @pl.when(k > 0)
        def _():
            col_factors(k - 1)
            load(k - 1).wait()
            tiles(k - 1)

        return 0

    lax.fori_loop(0, chunks, step, 0)
    col_relay(subs - 2)
    col_relay(subs - 1)
    row_factors(chunks - 1)
    col_factors(chunks - 1)
    load(chunks - 1).wait()

    for h in range(heads):
        row_sends(h, pan.at[h], row_recv.at[h, 0], lambda copy: copy.wait_send())

    @pl.when(is_source)
    def _():
        for d in range(n_x):
            col_copy(colp, colp, col_recv.at[0], d, r).wait_send()

    @pl.when(is_relay)
    def _():
        col_copy(colp, colp, col_recv.at[0], 0, r).wait_send()


def store_kernel(n_row, n_col, held, fac, colf, keep, out, late, last, late_sem, last_sem, sem):
    c = lax.axis_index("col")
    rows, cols = out.shape
    heads = P_SIZE // B
    ratio = n_col // n_row
    step_rows = 4 * ratio * B
    chunks = rows // step_rows
    group = chunks // SUPERS
    wide = cols // SUPERS
    step_blocks = step_rows // B
    q = SUPERS - 1
    first = (group - 1) * q

    def late_copy(i):
        part = (aligned(i, step_rows), pl.ds(q * wide, wide))
        return pltpu.make_async_copy(late.at[i % SLOTS], out.at[part], late_sem.at[i % SLOTS])

    def done_copy(i, j):
        part = (aligned(i, step_rows), pl.ds(j * wide, wide))
        return pltpu.make_async_copy(held.at[part], out.at[part], sem.at[i, j])

    def is_done(i, j):
        done = i < chunks - 1
        if j == q - 1:
            done = jnp.logical_and(done, jnp.logical_or(i < first, i >= first + q))
        return done

    def value(i, j):
        rows_at, cols_at = aligned(i, step_rows), aligned(j, wide)
        marks = keep[aligned(i, step_blocks), cols_at]
        return new_tile(held, fac, colf, marks, rows_at, cols_at, step_rows, wide)

    left = [(first + d, q - 1) for d in range(q)] + [(chunks - 1, j) for j in range(q)]

    def last_copy(m):
        i, j = left[m]
        part = (aligned(i, step_rows), pl.ds(j * wide, wide))
        return pltpu.make_async_copy(last.at[m], out.at[part], last_sem.at[m])

    def step(i, _):
        for j in range(q):
            @pl.when(is_done(i, j))
            def _():
                done_copy(i, j).start()

        @pl.when(i >= SLOTS)
        def _():
            late_copy(i - SLOTS).wait()

        late[i % SLOTS] = value(i, q)
        late_copy(i).start()
        return 0

    lax.fori_loop(0, chunks, step, 0)
    for m, (i, j) in enumerate(left):
        last[m] = value(i, j)
        if j == 0:
            @pl.when(c < heads)
            def _():
                last[m, :, 0:LANES] = head_lanes(
                    fac[aligned(i, step_rows), :], last[m, :, 0:LANES], c
                )
        last_copy(m).start()

    def drain(i, _):
        for j in range(q):
            @pl.when(is_done(i, j))
            def _():
                done_copy(i, j).wait()
        return 0

    lax.fori_loop(0, chunks, drain, 0)
    for i in range(max(chunks - SLOTS, 0), chunks):
        late_copy(i).wait()
    for m in range(len(left)):
        last_copy(m).wait()


def body(front, diag_inverse, fill_pattern):
    rows, cols = front.shape
    n_row = lax.axis_size("row")
    n_col = lax.axis_size("col")
    heads = P_SIZE // B
    ratio = n_col // n_row
    step_rows = 4 * ratio * B
    chunks = rows // step_rows
    subs = 2 * chunks
    inner = n_col // 4
    wide = cols // SUPERS
    bf16 = jnp.bfloat16
    any_space = pl.BlockSpec(memory_space=pl.ANY)
    vmem = pl.BlockSpec(memory_space=pltpu.VMEM)
    parts = pl.pallas_call(
        functools.partial(gather_kernel, n_row, n_col),
        out_shape=(
            pltpu.VMEM((rows, cols), bf16),
            pltpu.VMEM((rows, P_SIZE), bf16),
            pltpu.VMEM((P_SIZE, cols), bf16),
            pltpu.VMEM((rows // B, cols), jnp.float32),
        ),
        in_specs=[any_space, vmem, vmem],
        out_specs=(vmem,) * 4,
        scratch_shapes=[
            pltpu.VMEM((rows, LANES), bf16),
            pltpu.VMEM((heads, subs, ratio, B, LANES), bf16),
            pltpu.VMEM((subs, heads, B, LANES), bf16),
            pltpu.VMEM((P_SIZE, heads * LANES), bf16),
            pltpu.VMEM((P_SIZE, heads * LANES), bf16),
            pltpu.VMEM((rows // B, fill_pattern.shape[0]), bf16),
            pltpu.SemaphoreType.DMA((chunks,)),
            pltpu.SemaphoreType.DMA((2,)),
            pltpu.SemaphoreType.DMA((heads, subs)),
            pltpu.SemaphoreType.DMA((heads, inner + 1)),
            pltpu.SemaphoreType.DMA((subs,)),
            pltpu.SemaphoreType.DMA((n_row // 2,)),
        ],
        compiler_params=pltpu.CompilerParams(
            collective_id=0, has_side_effects=True, vmem_limit_bytes=14 * 2**20
        ),
        name="gather_update",
    )(front, diag_inverse, fill_pattern)
    held = [pltpu.with_memory_space_constraint(part, pltpu.VMEM) for part in parts]
    return pl.pallas_call(
        functools.partial(store_kernel, n_row, n_col),
        out_shape=jax.ShapeDtypeStruct((rows, cols), bf16),
        in_specs=[vmem] * 4,
        out_specs=any_space,
        scratch_shapes=[
            pltpu.VMEM((SLOTS, step_rows, wide), bf16),
            pltpu.VMEM((2 * (SUPERS - 1), step_rows, wide), bf16),
            pltpu.SemaphoreType.DMA((SLOTS,)),
            pltpu.SemaphoreType.DMA((2 * (SUPERS - 1),)),
            pltpu.SemaphoreType.DMA((chunks, SUPERS - 1)),
        ],
        compiler_params=pltpu.CompilerParams(vmem_limit_bytes=14 * 2**20),
        name="store",
    )(*held)


def solution(mesh):
    return jax.shard_map(
        body,
        mesh=mesh,
        in_specs=(P("row", "col"), P(), P()),
        out_specs=P("row", "col"),
        check_vma=False,
    )
```

```python
import functools

import jax
import jax.numpy as jnp
from jax import lax
from jax.experimental import pallas as pl
from jax.experimental.pallas import tpu as pltpu
from jax.sharding import PartitionSpec as P

B = 64
P_SIZE = 256
LANES = 128
SUPERS = 3
GROUP = 8
SPLIT = 2
AHEAD = 6
CHAIN = 3
LAG = 4
GLAG = 2
BURST = 4
SLOTS = 2
MESH = pl.DeviceIdType.MESH
NT = (((1,), (1,)), ((), ()))


def nt_dot(a, b):
    return lax.dot_general(a, b, NT, preferred_element_type=jnp.float32)


def nn_dot(a, b):
    return jnp.dot(a, b, preferred_element_type=jnp.float32)


def one_hot(shape, test):
    i = lax.broadcasted_iota(jnp.int32, shape, 0)
    j = lax.broadcasted_iota(jnp.int32, shape, 1)
    return jnp.where(test(i, j), 1.0, 0.0).astype(jnp.bfloat16)


def aligned(i, size):
    return pl.ds(pl.multiple_of(i * size, size), size)


class Plan:
    def __init__(self, n_row, n_col, rows, cols, c):
        self.heads = P_SIZE // B
        self.ratio = n_col // n_row
        self.group_rows = GROUP * B
        self.groups = rows // self.group_rows
        self.per = self.groups // self.ratio
        self.wide = cols // SUPERS
        self.subs = self.groups * SPLIT
        self.pieces = GROUP // 2 // SPLIT
        self.parity = c // n_row
        self.first = (self.ratio - 1 - self.parity) * self.per
        self.burst = jnp.where(self.first == 0, 1, BURST)

    def ready(self, j):
        return self.first + self.per // SUPERS * (j + 1) + GLAG

    def rows_done(self, j):
        return jnp.minimum(
            self.groups, self.burst * jnp.maximum(self.groups - self.ready(j), 0)
        )

    def place(self, g):
        return aligned(g % self.per, GROUP), self.ratio - 1 - g // self.per


def new_tile(plan, held, fac, colf, keep, g, j):
    cols_at = pl.ds(j * plan.wide, plan.wide)
    product = nn_dot(fac[aligned(g, plan.group_rows), :], colf[:, cols_at])
    marks = keep[aligned(g, GROUP), cols_at]
    masked = product.reshape(GROUP, B, plan.wide) * marks[:, None, :]
    return (held[g, :, :, cols_at].astype(jnp.float32) - masked).astype(jnp.bfloat16)


def head_lanes(fac_rows, old, c):
    to_front = one_hot((P_SIZE, LANES), lambda i, l: (i == c * B + l) & (l < B))
    piece = nn_dot(fac_rows, to_front).reshape(old.shape)
    lane = lax.broadcasted_iota(jnp.int32, old.shape, 2)
    return jnp.where(lane < B, piece, old.astype(jnp.float32)).astype(jnp.bfloat16)


def gather_kernel(
    n_row, n_col,
    front, diag, fill, out, fac, colf, keep,
    source, pan, colp, w_lo, w_hi, picked,
    load_sem, source_sem, row_recv, row_send, col_recv, col_send,
):
    r = lax.axis_index("row")
    c = lax.axis_index("col")
    rows, cols = fac.shape[0], colf.shape[1]
    plan = Plan(n_row, n_col, rows, cols, c)
    heads, ratio, groups, per, subs = plan.heads, plan.ratio, plan.groups, plan.per, plan.subs
    group_rows = plan.group_rows
    half = group_rows // 2
    outer, inner = 4, n_col // 4
    a = c // inner
    b = c % inner
    owner = c < heads
    x, core = r // 2, r % 2
    source_row = c % n_row
    source_x, source_core = source_row // 2, source_row % 2
    n_x = n_row // 2
    is_source = r == source_row
    is_relay = jnp.logical_and(core == source_core, x != source_x)
    col_subs = per * SPLIT
    col_first = plan.first * SPLIT

    def load(g):
        blocks, remainder = plan.place(g)
        return pltpu.make_async_copy(front.at[blocks, remainder], out.at[g], load_sem.at[g])

    def fetch(part):
        at = (pl.ds(0, GROUP), pl.ds(GROUP, (per - 1) * GROUP))[part]
        return pltpu.make_async_copy(
            front.at[at, :, :, 0:LANES], source.at[at], source_sem.at[part]
        )

    def row_copy(h, ref, recv, slot, target):
        return pltpu.make_async_remote_copy(
            src_ref=ref, dst_ref=ref,
            send_sem=row_send.at[h, slot], recv_sem=recv,
            device_id=(r, target), device_id_type=MESH,
        )

    def row_sends(h, ref, recv, act):
        a_h, b_h = h // inner, h % inner

        @pl.when(b == b_h)
        def _():
            @pl.when(jnp.logical_and(a >= a_h, a < outer - 1))
            def _():
                act(row_copy(h, ref, recv, 0, c + inner))

            @pl.when(jnp.logical_and(a <= a_h, a > 0))
            def _():
                act(row_copy(h, ref, recv, 1, c - inner))

            for d in range(1, inner):
                act(row_copy(h, ref, recv, 1 + d, a * inner + (b + d) % inner))

    def start(copy):
        copy.start()

    def own(s):
        for h in range(heads):
            @pl.when(c == h)
            def _():
                row_sends(h, pan.at[h, s], row_recv.at[h, s], start)

    def chain(s):
        for h in range(heads):
            @pl.when(jnp.logical_and(c != h, b == h % inner))
            def _():
                row_copy(h, pan.at[h, s], row_recv.at[h, s], 0, c).wait_recv()
                row_sends(h, pan.at[h, s], row_recv.at[h, s], start)

    def across(s):
        for h in range(heads):
            @pl.when(b != h % inner)
            def _():
                row_copy(h, pan.at[h, s], row_recv.at[h, s], 0, c).wait_recv()

    def col_copy(src, dst, recv, slot, target):
        return pltpu.make_async_remote_copy(
            src_ref=src, dst_ref=dst,
            send_sem=col_send.at[slot], recv_sem=recv,
            device_id=(target, c), device_id_type=MESH,
        )

    def col_local(s):
        return pltpu.make_async_copy(pan.at[:, col_first + s], colp.at[s], col_recv.at[s])

    def col_source(s):
        @pl.when(is_source & (s >= 0) & (s < col_subs))
        def _():
            src = pan.at[:, col_first + s]
            for d in range(1, n_x):
                target = ((x + d) % n_x) * 2 + core
                col_copy(src, colp.at[s], col_recv.at[s], d, target).start()
            col_copy(src, colp.at[s], col_recv.at[s], 0, x * 2 + 1 - core).start()
            col_local(s).start()

    def col_relay(s):
        @pl.when(is_relay & (s >= 0) & (s < col_subs))
        def _():
            copy = col_copy(colp.at[s], colp.at[s], col_recv.at[s], 0, x * 2 + 1 - core)
            copy.wait_recv()
            copy.start()

    def col_wait(s):
        @pl.when(is_source)
        def _():
            col_local(s).wait()

        @pl.when(jnp.logical_not(jnp.logical_or(is_source, is_relay)))
        def _():
            col_copy(colp.at[s], colp.at[s], col_recv.at[s], 0, r).wait_recv()

    @pl.when(owner)
    def _():
        fetch(0).start()
        fetch(1).start()

    barrier = pltpu.get_barrier_semaphore()

    @pl.when(a > 0)
    def _():
        pl.semaphore_signal(barrier, inc=1, device_id=(r, c - inner), device_id_type=MESH)

    @pl.when(a < outer - 1)
    def _():
        pl.semaphore_signal(barrier, inc=1, device_id=(r, c + inner), device_id_type=MESH)

    for d in range(1, inner):
        pl.semaphore_signal(
            barrier, inc=1, device_id=(r, a * inner + (b + d) % inner), device_id_type=MESH
        )
    for d in range(1, n_row):
        pl.semaphore_signal(barrier, inc=1, device_id=((r + d) % n_row, c), device_id_type=MESH)

    def pack(p, _):
        to_lo = one_hot((LANES, LANES), lambda i, j: (i == j) & (i < B))
        to_hi = one_hot((LANES, LANES), lambda i, j: (i + B == j) & (i < B))
        lo = source[pl.ds(p * GROUP, GROUP // 2)].reshape(ratio * half, LANES)
        hi = source[pl.ds(p * GROUP + GROUP // 2, GROUP // 2)].reshape(ratio * half, LANES)
        both = nn_dot(lo, to_lo) + nn_dot(hi, to_hi)
        both = both.astype(jnp.bfloat16).reshape(GROUP // 2, ratio, B, LANES)
        for parity in range(ratio):
            g = (ratio - 1 - parity) * per + p
            for i in range(SPLIT):
                at = i * plan.pieces
                pan[c, g * SPLIT + i] = both[at:at + plan.pieces, parity]
        return 0

    @pl.when(owner)
    def _():
        fetch(0).wait()
        pack(0, 0)

    extra = jnp.where(a > 0, 1, 0) + jnp.where(a < outer - 1, 1, 0)
    pl.semaphore_wait(barrier, inner - 1 + n_row - 1 + extra)

    for s in range(SPLIT):
        own(s)

    @pl.when(owner)
    def _():
        fetch(1).wait()
        lax.fori_loop(1, per, pack, 0)

    for s in range(SPLIT, AHEAD):
        own(s)
    for s in range(CHAIN):
        chain(s)

    def spread(shift):
        return one_hot(
            (P_SIZE, heads * LANES),
            lambda i, j: (i == (j // LANES) * B + j % LANES - shift)
            & (j % LANES >= shift) & (j % LANES < shift + B),
        )

    w_lo[...] = nn_dot(diag[...], spread(0)).astype(jnp.bfloat16)
    w_hi[...] = nn_dot(diag[...], spread(B)).astype(jnp.bfloat16)

    def row_block(i):
        g = i // GROUP
        local = ratio * (GROUP * (g % per) + i % GROUP) + ratio - 1 - g // per
        return local * n_row + r

    count = fill.shape[0]
    pick = one_hot((rows // B, count), lambda i, j: j == row_block(i))
    picked[...] = nn_dot(pick, fill[...].astype(jnp.float32).astype(jnp.bfloat16)).astype(
        jnp.bfloat16
    )

    def event(s):
        @pl.when(s + AHEAD < subs)
        def _():
            own(s + AHEAD)

        @pl.when(s + CHAIN < subs)
        def _():
            chain(s + CHAIN)

        across(s)
        col_source(s - col_first)
        col_relay(s - col_first - LAG)

    def row_factors(g):
        packed = jnp.concatenate(
            [pan[h, pl.ds(g * SPLIT, SPLIT)].reshape(half, LANES) for h in range(heads)],
            axis=1,
        )
        at = pl.multiple_of(g * group_rows, group_rows)
        fac[pl.ds(at, half), :] = nt_dot(packed, w_lo[...]).astype(jnp.bfloat16)
        fac[pl.ds(at + half, half), :] = nt_dot(packed, w_hi[...]).astype(jnp.bfloat16)

    def col_factors(g):
        for i in range(SPLIT):
            col_wait(g * SPLIT + i)
        packed = jnp.concatenate(
            [colp[pl.ds(g * SPLIT, SPLIT), h].reshape(half, LANES) for h in range(heads)],
            axis=1,
        )
        at = pl.multiple_of(g * group_rows, group_rows)
        colf[:, pl.ds(at, half)] = nt_dot(w_lo[...], packed).astype(jnp.bfloat16)
        colf[:, pl.ds(at + half, half)] = nt_dot(w_hi[...], packed).astype(jnp.bfloat16)

    def make_keep(g):
        at = pl.multiple_of(g * group_rows, group_rows)
        widen = one_hot(
            (count, group_rows), lambda i, l: i == ((at + l) // B) * n_col + c
        )
        marks = nn_dot(picked[...], widen)
        i = lax.broadcasted_iota(jnp.int32, marks.shape, 0)
        l = lax.broadcasted_iota(jnp.int32, marks.shape, 1)
        live = (row_block(i) >= heads) & (((at + l) // B) * n_col + c >= heads)
        keep[:, pl.ds(at, group_rows)] = jnp.where(live, marks, 0.0)

    def tiles(k, j):
        def one(m, _):
            g = plan.burst * (k - plan.ready(j)) + m
            out[g, :, :, pl.ds(j * plan.wide, plan.wide)] = new_tile(
                plan, out, fac, colf, keep, g, j
            )
            if j == 0:
                @pl.when(owner)
                def _():
                    out[g, :, :, 0:LANES] = head_lanes(
                        fac[aligned(g, group_rows), :], out[g, :, :, 0:LANES], c
                    )
            return 0

        lax.fori_loop(0, jnp.where(k >= plan.ready(j), plan.burst, 0), one, 0)

    def work(k, part):
        if part == 0:
            load(k).start()

            @pl.when(k > 0)
            def _():
                row_factors(k - 1)
                load(k - 1).wait()

            @pl.when(k < per)
            def _():
                make_keep(k)

            if SPLIT == 2:
                tiles(k, 0)
        elif part == SPLIT - 1:
            g = k - GLAG - plan.first

            @pl.when((g >= 0) & (g < per))
            def _():
                col_factors(g)

            tiles(k, 2)
            if SPLIT == 2:
                tiles(k, 1)
        elif part == 1:
            tiles(k, 0)
        elif part == 2:
            tiles(k, 1)

    def step(k, _):
        for i in range(SPLIT):
            event(k * SPLIT + i)
            work(k, i)
        return 0

    lax.fori_loop(0, groups, step, 0)

    for s in range(LAG):
        col_relay(subs - LAG - col_first + s)
    row_factors(groups - 1)
    for g in range(GLAG):
        @pl.when((groups - GLAG - plan.first + g < per))
        def _():
            col_factors(groups - GLAG - plan.first + g)
    load(groups - 1).wait()

    for h in range(heads):
        row_sends(h, pan.at[h], row_recv.at[h, 0], lambda copy: copy.wait_send())

    @pl.when(is_source)
    def _():
        for d in range(n_x):
            col_copy(colp, colp, col_recv.at[0], d, r).wait_send()

    @pl.when(is_relay)
    def _():
        col_copy(colp, colp, col_recv.at[0], 0, r).wait_send()


def store_kernel(n_row, n_col, held, fac, colf, keep, out, late, late_sem, sem):
    c = lax.axis_index("col")
    plan = Plan(n_row, n_col, fac.shape[0], colf.shape[1], c)
    wide = plan.wide

    def copy(g, j, done):
        cols_at = pl.ds(j * wide, wide)
        target = out.at[(*plan.place(g), slice(None), cols_at)]
        if done:
            return pltpu.make_async_copy(held.at[g, :, :, cols_at], target, sem.at[g, j])
        slot = g % SLOTS
        return pltpu.make_async_copy(late.at[j, slot], target, late_sem.at[j, slot])

    def step(g, _):
        for j in range(SUPERS):
            @pl.when(g < plan.rows_done(j))
            def _():
                copy(g, j, True).start()

        for j in range(SUPERS):
            @pl.when(g >= plan.rows_done(j))
            def _():
                slot = g % SLOTS

                @pl.when(g - SLOTS >= plan.rows_done(j))
                def _():
                    copy(g - SLOTS, j, False).wait()

                late[j, slot] = new_tile(plan, held, fac, colf, keep, g, j)
                if j == 0:
                    @pl.when(c < plan.heads)
                    def _():
                        late[j, slot, :, :, 0:LANES] = head_lanes(
                            fac[aligned(g, plan.group_rows), :],
                            late[j, slot, :, :, 0:LANES], c,
                        )
                copy(g, j, False).start()

        return 0

    lax.fori_loop(0, plan.groups, step, 0)

    def drain(g, _):
        for j in range(SUPERS):
            @pl.when(g < plan.rows_done(j))
            def _():
                copy(g, j, True).wait()

            @pl.when((g >= plan.rows_done(j)) & (g >= plan.groups - SLOTS))
            def _():
                copy(g, j, False).wait()
        return 0

    lax.fori_loop(0, plan.groups, drain, 0)


def body(front, diag_inverse, fill_pattern):
    rows, cols = front.shape
    n_row = lax.axis_size("row")
    n_col = lax.axis_size("col")
    plan = Plan(n_row, n_col, rows, cols, 0)
    heads, ratio, groups, subs = plan.heads, plan.ratio, plan.groups, plan.subs
    split = (groups * GROUP // ratio, ratio, B, cols)
    inner = n_col // 4
    bf16 = jnp.bfloat16
    any_space = pl.BlockSpec(memory_space=pl.ANY)
    vmem = pl.BlockSpec(memory_space=pltpu.VMEM)
    parts = pl.pallas_call(
        functools.partial(gather_kernel, n_row, n_col),
        out_shape=(
            pltpu.VMEM((groups, GROUP, B, cols), bf16),
            pltpu.VMEM((rows, P_SIZE), bf16),
            pltpu.VMEM((P_SIZE, cols), bf16),
            pltpu.VMEM((rows // B, cols), jnp.float32),
        ),
        in_specs=[any_space, vmem, vmem],
        out_specs=(vmem,) * 4,
        scratch_shapes=[
            pltpu.VMEM((*split[:3], LANES), bf16),
            pltpu.VMEM((heads, subs, plan.pieces, B, LANES), bf16),
            pltpu.VMEM((plan.per * SPLIT, heads, plan.pieces, B, LANES), bf16),
            pltpu.VMEM((P_SIZE, heads * LANES), bf16),
            pltpu.VMEM((P_SIZE, heads * LANES), bf16),
            pltpu.VMEM((rows // B, fill_pattern.shape[0]), bf16),
            pltpu.SemaphoreType.DMA((groups,)),
            pltpu.SemaphoreType.DMA((2,)),
            pltpu.SemaphoreType.DMA((heads, subs)),
            pltpu.SemaphoreType.DMA((heads, inner + 1)),
            pltpu.SemaphoreType.DMA((plan.per * SPLIT,)),
            pltpu.SemaphoreType.DMA((n_row // 2,)),
        ],
        compiler_params=pltpu.CompilerParams(
            collective_id=0, has_side_effects=True, vmem_limit_bytes=14 * 2**20
        ),
        name="gather_update",
    )(front.reshape(split), diag_inverse, fill_pattern)
    held = [pltpu.with_memory_space_constraint(part, pltpu.VMEM) for part in parts]
    result = pl.pallas_call(
        functools.partial(store_kernel, n_row, n_col),
        out_shape=jax.ShapeDtypeStruct(split, bf16),
        in_specs=[vmem] * 4,
        out_specs=any_space,
        scratch_shapes=[
            pltpu.VMEM((SUPERS, SLOTS, GROUP, B, plan.wide), bf16),
            pltpu.SemaphoreType.DMA((SUPERS, SLOTS)),
            pltpu.SemaphoreType.DMA((groups, SUPERS)),
        ],
        compiler_params=pltpu.CompilerParams(vmem_limit_bytes=14 * 2**20),
        name="store",
    )(*held)
    return result.reshape(rows, cols)


def solution(mesh):
    return jax.shard_map(
        body,
        mesh=mesh,
        in_specs=(P("row", "col"), P(), P()),
        out_specs=P("row", "col"),
        check_vma=False,
    )
```

```python
import functools

import jax
import jax.numpy as jnp
from jax import lax
from jax.experimental import pallas as pl
from jax.experimental.pallas import tpu as pltpu
from jax.sharding import PartitionSpec as P

B = 64
P_SIZE = 256
LANES = 128
SUPERS = 3
GROUP = 8
SPLIT = 2
AHEAD = 6
CHAIN = 3
LAG = 6
GLAG = 3
BURST = 2
QUIET = 0
SLOTS = 3
MESH = pl.DeviceIdType.MESH
NT = (((1,), (1,)), ((), ()))


def nt_dot(a, b):
    return lax.dot_general(a, b, NT, preferred_element_type=jnp.float32)


def nn_dot(a, b):
    return jnp.dot(a, b, preferred_element_type=jnp.float32)


def one_hot(shape, test):
    i = lax.broadcasted_iota(jnp.int32, shape, 0)
    j = lax.broadcasted_iota(jnp.int32, shape, 1)
    return jnp.where(test(i, j), 1.0, 0.0).astype(jnp.bfloat16)


def aligned(i, size):
    return pl.ds(pl.multiple_of(i * size, size), size)


class Plan:
    def __init__(self, n_row, n_col, rows, cols, c):
        self.heads = P_SIZE // B
        self.ratio = n_col // n_row
        self.group_rows = GROUP * B
        self.groups = rows // self.group_rows
        self.per = self.groups // self.ratio
        self.wide = cols // SUPERS
        self.subs = self.groups * SPLIT
        self.pieces = GROUP // 2 // SPLIT
        self.turn = self.ratio - 1 - c // n_row

    def mine(self, g):
        return (g >= 0) & (g % self.ratio == self.turn)

    def tiles_to(self, k, j):
        last = self.ratio * (self.per // SUPERS * (j + 1) - 1) + self.turn
        k = jnp.minimum(k, self.groups - 1 - QUIET)
        return jnp.clip(BURST * (k - last - GLAG), 0, jnp.maximum(k, 0))

    def rows_done(self, j):
        return self.tiles_to(self.groups, j)

    def place(self, g):
        return aligned(g // self.ratio, GROUP), self.ratio - 1 - g % self.ratio


def new_tile(plan, held, fac, colf, keep, g, j):
    cols_at = pl.ds(j * plan.wide, plan.wide)
    product = nn_dot(fac[aligned(g, plan.group_rows), :], colf[:, cols_at])
    marks = keep[aligned(g, GROUP), cols_at]
    masked = product.reshape(GROUP, B, plan.wide) * marks[:, None, :]
    return (held[g, :, :, cols_at].astype(jnp.float32) - masked).astype(jnp.bfloat16)


def gather_kernel(
    n_row, n_col,
    front, diag, fill, out, fac, colf, keep,
    source, pan, colp, w_lo, w_hi, picked,
    load_sem, source_sem, row_recv, row_send, col_recv, col_send,
):
    r = lax.axis_index("row")
    c = lax.axis_index("col")
    rows, cols = fac.shape[0], colf.shape[1]
    plan = Plan(n_row, n_col, rows, cols, c)
    heads, ratio, groups, per, subs = plan.heads, plan.ratio, plan.groups, plan.per, plan.subs
    group_rows = plan.group_rows
    half = group_rows // 2
    outer, inner = 4, n_col // 4
    a = c // inner
    b = c % inner
    owner = c < heads
    x, core = r // 2, r % 2
    source_row = c % n_row
    source_x, source_core = source_row // 2, source_row % 2
    n_x = n_row // 2
    is_source = r == source_row
    is_relay = jnp.logical_and(core == source_core, x != source_x)

    def col_slot(s):
        return s // SPLIT // ratio * SPLIT + s % SPLIT

    def load(g):
        blocks, remainder = plan.place(g)
        return pltpu.make_async_copy(front.at[blocks, remainder], out.at[g], load_sem.at[g])

    def fetch(part):
        at = (pl.ds(0, GROUP), pl.ds(GROUP, (per - 1) * GROUP))[part]
        return pltpu.make_async_copy(
            front.at[at, :, :, 0:LANES], source.at[at], source_sem.at[part]
        )

    def row_copy(h, ref, recv, slot, target):
        return pltpu.make_async_remote_copy(
            src_ref=ref, dst_ref=ref,
            send_sem=row_send.at[h, slot], recv_sem=recv,
            device_id=(r, target), device_id_type=MESH,
        )

    def row_sends(h, ref, recv, act):
        a_h, b_h = h // inner, h % inner

        @pl.when(b == b_h)
        def _():
            @pl.when(jnp.logical_and(a >= a_h, a < outer - 1))
            def _():
                act(row_copy(h, ref, recv, 0, c + inner))

            @pl.when(jnp.logical_and(a <= a_h, a > 0))
            def _():
                act(row_copy(h, ref, recv, 1, c - inner))

            for d in range(1, inner):
                act(row_copy(h, ref, recv, 1 + d, a * inner + (b + d) % inner))

    def start(copy):
        copy.start()

    def own(s):
        for h in range(heads):
            @pl.when(c == h)
            def _():
                row_sends(h, pan.at[h, s], row_recv.at[h, s], start)
                col_piece(h, s)

    def chain(h, s, when=True):
        @pl.when((c != h) & (b == h % inner) & when & (s < subs))
        def _():
            row_copy(h, pan.at[h, s], row_recv.at[h, s], 0, c).wait_recv()
            row_sends(h, pan.at[h, s], row_recv.at[h, s], start)
            col_piece(h, s)

    def near(h):
        return (a > h // inner) & (h // inner == (heads - 1) // inner)

    def across(s):
        for h in range(heads):
            @pl.when(b != h % inner)
            def _():
                row_copy(h, pan.at[h, s], row_recv.at[h, s], 0, c).wait_recv()
                col_piece(h, s)

    def col_piece(h, s):
        @pl.when(is_source & plan.mine(s // SPLIT))
        def _():
            t = col_slot(s)
            for d in range(1, n_x):
                target = ((x + d) % n_x) * 2 + core
                col_copy(pan.at[h, s], colp.at[t, h], col_recv.at[t], d, target).start()

    def col_copy(src, dst, recv, slot, target):
        return pltpu.make_async_remote_copy(
            src_ref=src, dst_ref=dst,
            send_sem=col_send.at[slot], recv_sem=recv,
            device_id=(target, c), device_id_type=MESH,
        )

    def col_local(s):
        t = col_slot(s)
        return pltpu.make_async_copy(pan.at[:, s], colp.at[t], col_recv.at[t])

    def col_mate(src, t):
        return col_copy(src, colp.at[t], col_recv.at[t], 0, x * 2 + 1 - core)

    def col_source(s):
        @pl.when(is_source & plan.mine(s // SPLIT))
        def _():
            col_mate(pan.at[:, s], col_slot(s)).start()
            col_local(s).start()

    def col_relay(s):
        @pl.when(is_relay & (s >= 0) & plan.mine(s // SPLIT))
        def _():
            copy = col_mate(colp.at[col_slot(s)], col_slot(s))
            copy.wait_recv()
            copy.start()

    def col_wait(s):
        @pl.when(is_source)
        def _():
            col_local(s).wait()

        @pl.when(jnp.logical_not(jnp.logical_or(is_source, is_relay)))
        def _():
            t = col_slot(s)
            col_copy(colp.at[t], colp.at[t], col_recv.at[t], 0, r).wait_recv()

    @pl.when(owner)
    def _():
        fetch(0).start()
        fetch(1).start()

    barrier = pltpu.get_barrier_semaphore()

    @pl.when(a > 0)
    def _():
        pl.semaphore_signal(barrier, inc=1, device_id=(r, c - inner), device_id_type=MESH)

    @pl.when(a < outer - 1)
    def _():
        pl.semaphore_signal(barrier, inc=1, device_id=(r, c + inner), device_id_type=MESH)

    for d in range(1, inner):
        pl.semaphore_signal(
            barrier, inc=1, device_id=(r, a * inner + (b + d) % inner), device_id_type=MESH
        )
    for d in range(1, n_row):
        pl.semaphore_signal(barrier, inc=1, device_id=((r + d) % n_row, c), device_id_type=MESH)

    def pack(p, _):
        to_lo = one_hot((LANES, LANES), lambda i, j: (i == j) & (i < B))
        to_hi = one_hot((LANES, LANES), lambda i, j: (i + B == j) & (i < B))
        lo = source[pl.ds(p * GROUP, GROUP // 2)].reshape(ratio * half, LANES)
        hi = source[pl.ds(p * GROUP + GROUP // 2, GROUP // 2)].reshape(ratio * half, LANES)
        both = nn_dot(lo, to_lo) + nn_dot(hi, to_hi)
        both = both.astype(jnp.bfloat16).reshape(GROUP // 2, ratio, B, LANES)
        for parity in range(ratio):
            g = p * ratio + ratio - 1 - parity
            for i in range(SPLIT):
                at = i * plan.pieces
                pan[c, g * SPLIT + i] = both[at:at + plan.pieces, parity]
        return 0

    @pl.when(owner)
    def _():
        fetch(0).wait()
        pack(0, 0)

    extra = jnp.where(a > 0, 1, 0) + jnp.where(a < outer - 1, 1, 0)
    pl.semaphore_wait(barrier, inner - 1 + n_row - 1 + extra)

    for s in range(SPLIT):
        own(s)

    @pl.when(owner)
    def _():
        fetch(1).wait()
        lax.fori_loop(1, per, pack, 0)

    for s in range(SPLIT, AHEAD):
        own(s)
    for h in reversed(range(heads)):
        for s in range(AHEAD):
            chain(h, s, near(h))
    for h in reversed(range(heads)):
        for s in range(CHAIN):
            chain(h, s, jnp.logical_not(near(h)))

    def spread(shift):
        return one_hot(
            (P_SIZE, heads * LANES),
            lambda i, j: (i == (j // LANES) * B + j % LANES - shift)
            & (j % LANES >= shift) & (j % LANES < shift + B),
        )

    w_lo[...] = nn_dot(diag[...], spread(0)).astype(jnp.bfloat16)
    w_hi[...] = nn_dot(diag[...], spread(B)).astype(jnp.bfloat16)

    def row_block(i):
        g = i // GROUP
        local = ratio * (GROUP * (g // ratio) + i % GROUP) + ratio - 1 - g % ratio
        return local * n_row + r

    count = fill.shape[0]
    pick = one_hot((rows // B, count), lambda i, j: j == row_block(i))
    picked[...] = nn_dot(pick, fill[...].astype(jnp.float32).astype(jnp.bfloat16)).astype(
        jnp.bfloat16
    )

    def event(s):
        @pl.when(s + AHEAD < subs)
        def _():
            own(s + AHEAD)

        for h in reversed(range(heads)):
            chain(h, s + jnp.where(near(h), AHEAD, CHAIN))

        across(s)
        col_source(s)
        col_relay(s - LAG)

    def row_factors(g):
        packed = jnp.concatenate(
            [pan[h, pl.ds(g * SPLIT, SPLIT)].reshape(half, LANES) for h in range(heads)],
            axis=1,
        )
        at = pl.multiple_of(g * group_rows, group_rows)
        fac[pl.ds(at, half), :] = nt_dot(packed, w_lo[...]).astype(jnp.bfloat16)
        fac[pl.ds(at + half, half), :] = nt_dot(packed, w_hi[...]).astype(jnp.bfloat16)

    def col_factors(g):
        for i in range(SPLIT):
            col_wait(g * SPLIT + i)
        p = g // ratio
        packed = jnp.concatenate(
            [colp[pl.ds(p * SPLIT, SPLIT), h].reshape(half, LANES) for h in range(heads)],
            axis=1,
        )
        at = pl.multiple_of(p * group_rows, group_rows)
        colf[:, pl.ds(at, half)] = nt_dot(w_lo[...], packed).astype(jnp.bfloat16)
        colf[:, pl.ds(at + half, half)] = nt_dot(w_hi[...], packed).astype(jnp.bfloat16)

        @pl.when(owner & (p == 0))
        def _():
            unit = one_hot((P_SIZE, LANES), lambda i, l: i == c * B + l)
            lane = lax.broadcasted_iota(jnp.int32, unit.shape, 1)
            colf[:, 0:LANES] = jnp.where(lane < B, -unit, colf[:, 0:LANES])

    def clear(g):
        @pl.when(owner)
        def _():
            old = out[g, :, :, 0:LANES]
            lane = lax.broadcasted_iota(jnp.int32, old.shape, 2)
            out[g, :, :, 0:LANES] = jnp.where(lane < B, jnp.zeros_like(old), old)

    def make_keep(g):
        at = pl.multiple_of(g * group_rows, group_rows)
        widen = one_hot(
            (count, group_rows), lambda i, l: i == ((at + l) // B) * n_col + c
        )
        marks = nn_dot(picked[...], widen)
        i = lax.broadcasted_iota(jnp.int32, marks.shape, 0)
        l = lax.broadcasted_iota(jnp.int32, marks.shape, 1)
        marks = jnp.where(row_block(i) >= heads, marks, 0.0)
        head = ((at + l) // B) * n_col + c < heads
        keep[:, pl.ds(at, group_rows)] = jnp.where(head, 1.0, marks)

    def tile(g, j):
        out[g, :, :, pl.ds(j * plan.wide, plan.wide)] = new_tile(
            plan, out, fac, colf, keep, g, j
        )

    def tiles(k, j):
        def one(g, _):
            tile(g, j)
            return 0

        lax.fori_loop(plan.tiles_to(k - 1, j), plan.tiles_to(k, j), one, 0)

    def work(k, part):
        if part == 0:
            load(k).start()

            @pl.when(k > 0)
            def _():
                row_factors(k - 1)
                load(k - 1).wait()
                clear(k - 1)

            @pl.when(k < per)
            def _():
                make_keep(k)

            if SPLIT == 2:
                tiles(k, 0)
        elif part == SPLIT - 1:
            @pl.when(plan.mine(k - GLAG))
            def _():
                col_factors(k - GLAG)

            tiles(k, 2)
            if SPLIT == 2:
                tiles(k, 1)
        elif part == 1:
            tiles(k, 0)
        elif part == 2:
            tiles(k, 1)

    def step(k, _):
        for i in range(SPLIT):
            event(k * SPLIT + i)
            work(k, i)
        return 0

    lax.fori_loop(0, groups, step, 0)

    row_factors(groups - 1)
    load(groups - 1).wait()
    clear(groups - 1)
    for i in range(LAG):
        col_relay(subs - LAG + i)
    for i in range(GLAG):
        @pl.when(plan.mine(groups - GLAG + i))
        def _():
            col_factors(groups - GLAG + i)

    for h in range(heads):
        row_sends(h, pan.at[h], row_recv.at[h, 0], lambda copy: copy.wait_send())

    @pl.when(is_source)
    def _():
        for d in range(n_x):
            col_copy(colp, colp, col_recv.at[0], d, r).wait_send()

    @pl.when(is_relay)
    def _():
        col_copy(colp, colp, col_recv.at[0], 0, r).wait_send()


def store_kernel(n_row, n_col, held, fac, colf, keep, out, late, late_sem, sem):
    c = lax.axis_index("col")
    plan = Plan(n_row, n_col, fac.shape[0], colf.shape[1], c)
    wide = plan.wide

    def copy(g, j, done):
        cols_at = pl.ds(j * wide, wide)
        target = out.at[(*plan.place(g), slice(None), cols_at)]
        if done:
            return pltpu.make_async_copy(held.at[g, :, :, cols_at], target, sem.at[g, j])
        slot = g % SLOTS
        return pltpu.make_async_copy(late.at[j, slot], target, late_sem.at[j, slot])

    def step(i, _):
        for j in range(SUPERS):
            @pl.when(i < plan.rows_done(j))
            def _():
                copy(i, j, True).start()

        g = plan.groups - 1 - i
        for j in range(SUPERS):
            @pl.when(g >= plan.rows_done(j))
            def _():
                slot = g % SLOTS

                @pl.when(i >= SLOTS)
                def _():
                    copy(g + SLOTS, j, False).wait()

                late[j, slot] = new_tile(plan, held, fac, colf, keep, g, j)
                copy(g, j, False).start()

        return 0

    lax.fori_loop(0, plan.groups, step, 0)

    def drain(g, _):
        for j in range(SUPERS):
            @pl.when(g < plan.rows_done(j))
            def _():
                copy(g, j, True).wait()

            @pl.when((g >= plan.rows_done(j)) & (g < plan.rows_done(j) + SLOTS))
            def _():
                copy(g, j, False).wait()
        return 0

    lax.fori_loop(0, plan.groups, drain, 0)


def body(front, diag_inverse, fill_pattern):
    rows, cols = front.shape
    n_row = lax.axis_size("row")
    n_col = lax.axis_size("col")
    plan = Plan(n_row, n_col, rows, cols, 0)
    heads, ratio, groups, subs = plan.heads, plan.ratio, plan.groups, plan.subs
    split = (groups * GROUP // ratio, ratio, B, cols)
    inner = n_col // 4
    bf16 = jnp.bfloat16
    any_space = pl.BlockSpec(memory_space=pl.ANY)
    vmem = pl.BlockSpec(memory_space=pltpu.VMEM)
    parts = pl.pallas_call(
        functools.partial(gather_kernel, n_row, n_col),
        out_shape=(
            pltpu.VMEM((groups, GROUP, B, cols), bf16),
            pltpu.VMEM((rows, P_SIZE), bf16),
            pltpu.VMEM((P_SIZE, cols), bf16),
            pltpu.VMEM((rows // B, cols), jnp.float32),
        ),
        in_specs=[any_space, vmem, vmem],
        out_specs=(vmem,) * 4,
        scratch_shapes=[
            pltpu.VMEM((*split[:3], LANES), bf16),
            pltpu.VMEM((heads, subs, plan.pieces, B, LANES), bf16),
            pltpu.VMEM((plan.per * SPLIT, heads, plan.pieces, B, LANES), bf16),
            pltpu.VMEM((P_SIZE, heads * LANES), bf16),
            pltpu.VMEM((P_SIZE, heads * LANES), bf16),
            pltpu.VMEM((rows // B, fill_pattern.shape[0]), bf16),
            pltpu.SemaphoreType.DMA((groups,)),
            pltpu.SemaphoreType.DMA((2,)),
            pltpu.SemaphoreType.DMA((heads, subs)),
            pltpu.SemaphoreType.DMA((heads, inner + 1)),
            pltpu.SemaphoreType.DMA((plan.per * SPLIT,)),
            pltpu.SemaphoreType.DMA((n_row // 2,)),
        ],
        compiler_params=pltpu.CompilerParams(
            collective_id=0, has_side_effects=True, vmem_limit_bytes=14 * 2**20
        ),
        name="gather_update",
    )(front.reshape(split), diag_inverse, fill_pattern)
    held = [pltpu.with_memory_space_constraint(part, pltpu.VMEM) for part in parts]
    result = pl.pallas_call(
        functools.partial(store_kernel, n_row, n_col),
        out_shape=jax.ShapeDtypeStruct(split, bf16),
        in_specs=[vmem] * 4,
        out_specs=any_space,
        scratch_shapes=[
            pltpu.VMEM((SUPERS, SLOTS, GROUP, B, plan.wide), bf16),
            pltpu.SemaphoreType.DMA((SUPERS, SLOTS)),
            pltpu.SemaphoreType.DMA((groups, SUPERS)),
        ],
        compiler_params=pltpu.CompilerParams(vmem_limit_bytes=14 * 2**20),
        name="store",
    )(*held)
    return result.reshape(rows, cols)


def solution(mesh):
    return jax.shard_map(
        body,
        mesh=mesh,
        in_specs=(P("row", "col"), P(), P()),
        out_specs=P("row", "col"),
        check_vma=False,
    )
```

```python
import functools

import jax
import jax.numpy as jnp
from jax import lax
from jax.experimental import pallas as pl
from jax.experimental.pallas import tpu as pltpu
from jax.sharding import PartitionSpec as P

B = 64
P_SIZE = 256
LANES = 128
SUPERS = 3
GROUP = 8
SPLIT = 2
AHEAD = 4
CROSS = 10
CHAIN = 3
LAG = 4
GLAG = 2
BURST = 2
QUIET = 1
PRELOAD = 6
SLOTS = 3
MESH = pl.DeviceIdType.MESH
NT = (((1,), (1,)), ((), ()))


def nt_dot(a, b):
    return lax.dot_general(a, b, NT, preferred_element_type=jnp.float32)


def nn_dot(a, b):
    return jnp.dot(a, b, preferred_element_type=jnp.float32)


def one_hot(shape, test):
    i = lax.broadcasted_iota(jnp.int32, shape, 0)
    j = lax.broadcasted_iota(jnp.int32, shape, 1)
    return jnp.where(test(i, j), 1.0, 0.0).astype(jnp.bfloat16)


def aligned(i, size):
    return pl.ds(pl.multiple_of(i * size, size), size)


class Plan:
    def __init__(self, n_row, n_col, rows, cols, c):
        self.heads = P_SIZE // B
        self.ratio = n_col // n_row
        self.group_rows = GROUP * B
        self.groups = rows // self.group_rows
        self.per = self.groups // self.ratio
        self.wide = cols // SUPERS
        self.subs = self.groups * SPLIT
        self.pieces = GROUP // 2 // SPLIT
        self.turn = self.ratio - 1 - c // n_row

    def swap(self, g):
        low, high = self.groups - 3, self.groups - 2
        return jnp.where(g == low, high, jnp.where(g == high, low, g))

    def mine(self, g):
        return (g >= 0) & (self.swap(g) % self.ratio == self.turn)

    def tiles_to(self, k, j):
        last = self.swap(self.ratio * (self.per // SUPERS * (j + 1) - 1) + self.turn)
        k = jnp.minimum(k, self.groups - 1 - QUIET)
        return jnp.clip(BURST * (k - last - GLAG), 0, jnp.maximum(k, 0))

    def rows_done(self, j):
        return self.tiles_to(self.groups, j)

    def place(self, g):
        turn = self.swap(g)
        return aligned(turn // self.ratio, GROUP), self.ratio - 1 - turn % self.ratio


def new_tile(plan, held, fac, colf, keep, g, j):
    cols_at = pl.ds(j * plan.wide, plan.wide)
    product = nn_dot(fac[aligned(g, plan.group_rows), :], colf[:, cols_at])
    marks = keep[aligned(g, GROUP), cols_at]
    masked = product.reshape(GROUP, B, plan.wide) * marks[:, None, :]
    return (held[g, :, :, cols_at].astype(jnp.float32) - masked).astype(jnp.bfloat16)


def gather_kernel(
    n_row, n_col,
    front, diag, fill, out, fac, colf, keep,
    source, pan, colp, w_lo, w_hi, picked,
    load_sem, source_sem, row_recv, row_send, col_recv, col_send,
):
    r = lax.axis_index("row")
    c = lax.axis_index("col")
    rows, cols = fac.shape[0], colf.shape[1]
    plan = Plan(n_row, n_col, rows, cols, c)
    heads, ratio, groups, per, subs = plan.heads, plan.ratio, plan.groups, plan.per, plan.subs
    group_rows = plan.group_rows
    half = group_rows // 2
    outer, inner = 4, n_col // 4
    a = c // inner
    b = c % inner
    owner = c < heads
    x, core = r // 2, r % 2
    source_row = c % n_row
    source_x, source_core = source_row // 2, source_row % 2
    n_x = n_row // 2
    is_source = r == source_row
    is_relay = jnp.logical_and(core == source_core, x != source_x)

    def col_slot(s):
        return plan.swap(s // SPLIT) // ratio * SPLIT + s % SPLIT

    def load(g):
        blocks, remainder = plan.place(g)
        return pltpu.make_async_copy(front.at[blocks, remainder], out.at[g], load_sem.at[g])

    def fetch(part):
        at = (pl.ds(0, GROUP), pl.ds(GROUP, (per - 1) * GROUP))[part]
        return pltpu.make_async_copy(
            front.at[at, :, :, 0:LANES], source.at[at], source_sem.at[part]
        )

    def row_copy(h, ref, recv, slot, target):
        return pltpu.make_async_remote_copy(
            src_ref=ref, dst_ref=ref,
            send_sem=row_send.at[h, slot], recv_sem=recv,
            device_id=(r, target), device_id_type=MESH,
        )

    slots = tuple(range(inner + 1))

    def row_sends(h, ref, recv, act, slots=slots):
        a_h, b_h = h // inner, h % inner

        @pl.when(b == b_h)
        def _():
            if 0 in slots:
                @pl.when(jnp.logical_and(a >= a_h, a < outer - 1))
                def _():
                    act(row_copy(h, ref, recv, 0, c + inner))

            if 1 in slots:
                @pl.when(jnp.logical_and(a <= a_h, a > 0))
                def _():
                    act(row_copy(h, ref, recv, 1, c - inner))

            for d in range(1, inner):
                if 1 + d in slots:
                    act(row_copy(h, ref, recv, 1 + d, a * inner + (b + d) % inner))

    def start(copy):
        copy.start()

    def cross(h):
        top = (heads - 1) // inner
        if top == 0:
            return ()
        return (0,) if h // inner < top else (1,)

    def own(s):
        for h in range(heads):
            @pl.when((c == h) & (s < subs))
            def _():
                rest = tuple(slot for slot in slots if slot not in cross(h))
                row_sends(h, pan.at[h, s], row_recv.at[h, s], start, rest)
                col_piece(h, s)

    def own_cross(s):
        for h in range(heads):
            @pl.when((c == h) & (s < subs))
            def _():
                row_sends(h, pan.at[h, s], row_recv.at[h, s], start, cross(h))

    def chain(h, s, when=True):
        @pl.when((c != h) & (b == h % inner) & when & (s < subs))
        def _():
            row_copy(h, pan.at[h, s], row_recv.at[h, s], 0, c).wait_recv()
            row_sends(h, pan.at[h, s], row_recv.at[h, s], start)
            col_piece(h, s)

    def near(h):
        return (a > h // inner) & (h // inner == (heads - 1) // inner)

    def across(s):
        for h in range(heads):
            @pl.when(b != h % inner)
            def _():
                row_copy(h, pan.at[h, s], row_recv.at[h, s], 0, c).wait_recv()
                col_piece(h, s)

    def col_piece(h, s):
        @pl.when(is_source & plan.mine(s // SPLIT))
        def _():
            t = col_slot(s)
            for d in range(1, n_x):
                target = ((x + d) % n_x) * 2 + core
                col_copy(pan.at[h, s], colp.at[t, h], col_recv.at[t], d, target).start()

    def col_copy(src, dst, recv, slot, target):
        return pltpu.make_async_remote_copy(
            src_ref=src, dst_ref=dst,
            send_sem=col_send.at[slot], recv_sem=recv,
            device_id=(target, c), device_id_type=MESH,
        )

    def col_local(s):
        t = col_slot(s)
        return pltpu.make_async_copy(pan.at[:, s], colp.at[t], col_recv.at[t])

    def col_mate(src, t):
        return col_copy(src, colp.at[t], col_recv.at[t], 0, x * 2 + 1 - core)

    def col_source(s):
        @pl.when(is_source & plan.mine(s // SPLIT))
        def _():
            col_mate(pan.at[:, s], col_slot(s)).start()
            col_local(s).start()

    def col_relay(s):
        @pl.when(is_relay & (s >= 0) & plan.mine(s // SPLIT))
        def _():
            copy = col_mate(colp.at[col_slot(s)], col_slot(s))
            copy.wait_recv()
            copy.start()

    def col_wait(s):
        @pl.when(is_source)
        def _():
            col_local(s).wait()

        @pl.when(jnp.logical_not(jnp.logical_or(is_source, is_relay)))
        def _():
            t = col_slot(s)
            col_copy(colp.at[t], colp.at[t], col_recv.at[t], 0, r).wait_recv()

    @pl.when(owner)
    def _():
        fetch(0).start()
        fetch(1).start()

    early = jnp.where(owner, 0, min(PRELOAD, groups))
    lax.fori_loop(0, early, lambda g, _: (load(g).start(), 0)[1], 0)

    barrier = pltpu.get_barrier_semaphore()

    @pl.when(a > 0)
    def _():
        pl.semaphore_signal(barrier, inc=1, device_id=(r, c - inner), device_id_type=MESH)

    @pl.when(a < outer - 1)
    def _():
        pl.semaphore_signal(barrier, inc=1, device_id=(r, c + inner), device_id_type=MESH)

    for d in range(1, inner):
        pl.semaphore_signal(
            barrier, inc=1, device_id=(r, a * inner + (b + d) % inner), device_id_type=MESH
        )
    for d in range(1, n_row):
        pl.semaphore_signal(barrier, inc=1, device_id=((r + d) % n_row, c), device_id_type=MESH)

    def pack(p, _):
        to_lo = one_hot((LANES, LANES), lambda i, j: (i == j) & (i < B))
        to_hi = one_hot((LANES, LANES), lambda i, j: (i + B == j) & (i < B))
        lo = source[pl.ds(p * GROUP, GROUP // 2)].reshape(ratio * half, LANES)
        hi = source[pl.ds(p * GROUP + GROUP // 2, GROUP // 2)].reshape(ratio * half, LANES)
        both = nn_dot(lo, to_lo) + nn_dot(hi, to_hi)
        both = both.astype(jnp.bfloat16).reshape(GROUP // 2, ratio, B, LANES)
        for parity in range(ratio):
            g = plan.swap(p * ratio + ratio - 1 - parity)
            for i in range(SPLIT):
                at = i * plan.pieces
                pan[c, g * SPLIT + i] = both[at:at + plan.pieces, parity]
        return 0

    @pl.when(owner)
    def _():
        fetch(0).wait()
        pack(0, 0)

    extra = jnp.where(a > 0, 1, 0) + jnp.where(a < outer - 1, 1, 0)
    pl.semaphore_wait(barrier, inner - 1 + n_row - 1 + extra)

    sent = SPLIT * ratio
    for s in range(sent):
        if s < AHEAD:
            own(s)
        if s < CROSS:
            own_cross(s)

    @pl.when(owner)
    def _():
        fetch(1).wait()
        lax.fori_loop(1, per, pack, 0)

    for s in range(sent, max(AHEAD, CROSS)):
        if s < AHEAD:
            own(s)
        if s < CROSS:
            own_cross(s)
    for h in reversed(range(heads)):
        for s in range(AHEAD):
            chain(h, s, near(h))
    for h in reversed(range(heads)):
        for s in range(CHAIN):
            chain(h, s, jnp.logical_not(near(h)))

    def spread(shift):
        return one_hot(
            (P_SIZE, heads * LANES),
            lambda i, j: (i == (j // LANES) * B + j % LANES - shift)
            & (j % LANES >= shift) & (j % LANES < shift + B),
        )

    w_lo[...] = nn_dot(diag[...], spread(0)).astype(jnp.bfloat16)
    w_hi[...] = nn_dot(diag[...], spread(B)).astype(jnp.bfloat16)

    def row_block(i):
        g = plan.swap(i // GROUP)
        local = ratio * (GROUP * (g // ratio) + i % GROUP) + ratio - 1 - g % ratio
        return local * n_row + r

    count = fill.shape[0]
    pick = one_hot((rows // B, count), lambda i, j: j == row_block(i))
    picked[...] = nn_dot(pick, fill[...].astype(jnp.float32).astype(jnp.bfloat16)).astype(
        jnp.bfloat16
    )

    def event(s):
        own(s + AHEAD)
        own_cross(s + CROSS)
        for h in reversed(range(heads)):
            chain(h, s + jnp.where(near(h), AHEAD, CHAIN))

        across(s)
        col_source(s)
        col_relay(s - LAG)

    def row_factors(g):
        packed = jnp.concatenate(
            [pan[h, pl.ds(g * SPLIT, SPLIT)].reshape(half, LANES) for h in range(heads)],
            axis=1,
        )
        at = pl.multiple_of(g * group_rows, group_rows)
        fac[pl.ds(at, half), :] = nt_dot(packed, w_lo[...]).astype(jnp.bfloat16)
        fac[pl.ds(at + half, half), :] = nt_dot(packed, w_hi[...]).astype(jnp.bfloat16)

    def col_factors(g):
        for i in range(SPLIT):
            col_wait(g * SPLIT + i)
        p = plan.swap(g) // ratio
        packed = jnp.concatenate(
            [colp[pl.ds(p * SPLIT, SPLIT), h].reshape(half, LANES) for h in range(heads)],
            axis=1,
        )
        at = pl.multiple_of(p * group_rows, group_rows)
        colf[:, pl.ds(at, half)] = nt_dot(w_lo[...], packed).astype(jnp.bfloat16)
        colf[:, pl.ds(at + half, half)] = nt_dot(w_hi[...], packed).astype(jnp.bfloat16)

        @pl.when(owner & (p == 0))
        def _():
            unit = one_hot((P_SIZE, LANES), lambda i, l: i == c * B + l)
            lane = lax.broadcasted_iota(jnp.int32, unit.shape, 1)
            colf[:, 0:LANES] = jnp.where(lane < B, -unit, colf[:, 0:LANES])

    def clear(g):
        @pl.when(owner)
        def _():
            old = out[g, :, :, 0:LANES]
            lane = lax.broadcasted_iota(jnp.int32, old.shape, 2)
            out[g, :, :, 0:LANES] = jnp.where(lane < B, jnp.zeros_like(old), old)

    def make_keep(g):
        at = pl.multiple_of(g * group_rows, group_rows)
        widen = one_hot(
            (count, group_rows), lambda i, l: i == ((at + l) // B) * n_col + c
        )
        marks = nn_dot(picked[...], widen)
        i = lax.broadcasted_iota(jnp.int32, marks.shape, 0)
        l = lax.broadcasted_iota(jnp.int32, marks.shape, 1)
        marks = jnp.where(row_block(i) >= heads, marks, 0.0)
        head = ((at + l) // B) * n_col + c < heads
        keep[:, pl.ds(at, group_rows)] = jnp.where(head, 1.0, marks)

    def tile(g, j):
        out[g, :, :, pl.ds(j * plan.wide, plan.wide)] = new_tile(
            plan, out, fac, colf, keep, g, j
        )

    def tiles(k, j):
        def one(g, _):
            tile(g, j)
            return 0

        lax.fori_loop(plan.tiles_to(k - 1, j), plan.tiles_to(k, j), one, 0)

    def work(k, part):
        if part == 0:
            @pl.when(k + early < groups)
            def _():
                load(k + early).start()

            @pl.when(k > 0)
            def _():
                row_factors(k - 1)
                load(k - 1).wait()
                clear(k - 1)

            @pl.when(k < per)
            def _():
                make_keep(k)

            if SPLIT == 2:
                tiles(k, 0)
        elif part == SPLIT - 1:
            @pl.when(plan.mine(k - GLAG))
            def _():
                col_factors(k - GLAG)

            tiles(k, 2)
            if SPLIT == 2:
                tiles(k, 1)
        elif part == 1:
            tiles(k, 0)
        elif part == 2:
            tiles(k, 1)

    def step(k, _):
        for i in range(SPLIT):
            event(k * SPLIT + i)
            work(k, i)
        return 0

    lax.fori_loop(0, groups, step, 0)

    row_factors(groups - 1)
    load(groups - 1).wait()
    clear(groups - 1)
    for i in range(LAG):
        col_relay(subs - LAG + i)
    for i in range(GLAG):
        @pl.when(plan.mine(groups - GLAG + i))
        def _():
            col_factors(groups - GLAG + i)

    for h in range(heads):
        row_sends(h, pan.at[h], row_recv.at[h, 0], lambda copy: copy.wait_send())

    @pl.when(is_source)
    def _():
        for d in range(n_x):
            col_copy(colp, colp, col_recv.at[0], d, r).wait_send()

    @pl.when(is_relay)
    def _():
        col_copy(colp, colp, col_recv.at[0], 0, r).wait_send()


def store_kernel(n_row, n_col, held, fac, colf, keep, out, late, late_sem, sem):
    c = lax.axis_index("col")
    plan = Plan(n_row, n_col, fac.shape[0], colf.shape[1], c)
    wide = plan.wide

    def copy(g, j, done):
        cols_at = pl.ds(j * wide, wide)
        target = out.at[(*plan.place(g), slice(None), cols_at)]
        if done:
            return pltpu.make_async_copy(held.at[g, :, :, cols_at], target, sem.at[g, j])
        slot = g % SLOTS
        return pltpu.make_async_copy(late.at[j, slot], target, late_sem.at[j, slot])

    def step(i, _):
        for j in range(SUPERS):
            @pl.when(i < plan.rows_done(j))
            def _():
                copy(i, j, True).start()

        g = plan.groups - 1 - i
        for j in range(SUPERS):
            @pl.when(g >= plan.rows_done(j))
            def _():
                slot = g % SLOTS

                @pl.when(i >= SLOTS)
                def _():
                    copy(g + SLOTS, j, False).wait()

                late[j, slot] = new_tile(plan, held, fac, colf, keep, g, j)
                copy(g, j, False).start()

        return 0

    lax.fori_loop(0, plan.groups, step, 0)

    def drain(g, _):
        for j in range(SUPERS):
            @pl.when(g < plan.rows_done(j))
            def _():
                copy(g, j, True).wait()

            @pl.when((g >= plan.rows_done(j)) & (g < plan.rows_done(j) + SLOTS))
            def _():
                copy(g, j, False).wait()
        return 0

    lax.fori_loop(0, plan.groups, drain, 0)


def body(front, diag_inverse, fill_pattern):
    rows, cols = front.shape
    n_row = lax.axis_size("row")
    n_col = lax.axis_size("col")
    plan = Plan(n_row, n_col, rows, cols, 0)
    heads, ratio, groups, subs = plan.heads, plan.ratio, plan.groups, plan.subs
    split = (groups * GROUP // ratio, ratio, B, cols)
    inner = n_col // 4
    bf16 = jnp.bfloat16
    any_space = pl.BlockSpec(memory_space=pl.ANY)
    vmem = pl.BlockSpec(memory_space=pltpu.VMEM)
    parts = pl.pallas_call(
        functools.partial(gather_kernel, n_row, n_col),
        out_shape=(
            pltpu.VMEM((groups, GROUP, B, cols), bf16),
            pltpu.VMEM((rows, P_SIZE), bf16),
            pltpu.VMEM((P_SIZE, cols), bf16),
            pltpu.VMEM((rows // B, cols), jnp.float32),
        ),
        in_specs=[any_space, vmem, vmem],
        out_specs=(vmem,) * 4,
        scratch_shapes=[
            pltpu.VMEM((*split[:3], LANES), bf16),
            pltpu.VMEM((heads, subs, plan.pieces, B, LANES), bf16),
            pltpu.VMEM((plan.per * SPLIT, heads, plan.pieces, B, LANES), bf16),
            pltpu.VMEM((P_SIZE, heads * LANES), bf16),
            pltpu.VMEM((P_SIZE, heads * LANES), bf16),
            pltpu.VMEM((rows // B, fill_pattern.shape[0]), bf16),
            pltpu.SemaphoreType.DMA((groups,)),
            pltpu.SemaphoreType.DMA((2,)),
            pltpu.SemaphoreType.DMA((heads, subs)),
            pltpu.SemaphoreType.DMA((heads, inner + 1)),
            pltpu.SemaphoreType.DMA((plan.per * SPLIT,)),
            pltpu.SemaphoreType.DMA((n_row // 2,)),
        ],
        compiler_params=pltpu.CompilerParams(
            collective_id=0, has_side_effects=True, vmem_limit_bytes=14 * 2**20
        ),
        name="gather_update",
    )(front.reshape(split), diag_inverse, fill_pattern)
    held = [pltpu.with_memory_space_constraint(part, pltpu.VMEM) for part in parts]
    result = pl.pallas_call(
        functools.partial(store_kernel, n_row, n_col),
        out_shape=jax.ShapeDtypeStruct(split, bf16),
        in_specs=[vmem] * 4,
        out_specs=any_space,
        scratch_shapes=[
            pltpu.VMEM((SUPERS, SLOTS, GROUP, B, plan.wide), bf16),
            pltpu.SemaphoreType.DMA((SUPERS, SLOTS)),
            pltpu.SemaphoreType.DMA((groups, SUPERS)),
        ],
        compiler_params=pltpu.CompilerParams(vmem_limit_bytes=14 * 2**20),
        name="store",
    )(*held)
    return result.reshape(rows, cols)


def solution(mesh):
    return jax.shard_map(
        body,
        mesh=mesh,
        in_specs=(P("row", "col"), P(), P()),
        out_specs=P("row", "col"),
        check_vma=False,
    )
```
